32 devices in a mesh: sample: 4 (over y, x), fsdp: 8 (over z, core).
Axes of the slice: x: 2, y: 2, z: 4, core: 2. Of those that a mesh axis runs over, the one named last changes fastest.
Arguments:
- seed_step: int32 [2], replicated, may hold values from 0 to 16777215
- attn: bfloat16 [16384, 2048], P(('sample', 'fsdp')), may hold values from -6 to 6
- resid: bfloat16 [16384, 4096], P(('sample', 'fsdp')), may hold values from -36 to 36
- cotangent: bfloat16 [16384, 4096], P(('sample', 'fsdp')), may hold values from -6 to 6
- gain: bfloat16 [4096], replicated, may hold values from 0.099609375 to 1.8984375
- mean: float32 [2048, 4096], P('fsdp'), may hold values from -6 to 6
- hess: float32 [2048, 4096], P('fsdp'), may hold values from 0.25 to 4
- momentum: float32 [2048, 4096], P('fsdp'), may hold values from -3 to 3
Outputs:
- new_mean: float32 [2048, 4096], P('fsdp')
- new_hess: float32 [2048, 4096], P('fsdp')
- new_momentum: float32 [2048, 4096], P('fsdp')
The draws below stay inside these ranges and needn't reach their ends.
All inputs are finite; a program needn't handle non-finite values.
Results may differ from the reference program's by a relative error of at most 0.0035.
Values may be sent and summed in bfloat16 or wider, within the bound.
A program may use at most 192 MiB of HBM per device.

```python
import math
import jax
import jax.numpy as jnp
from jax import lax

D = 4096
IN = 2048
TOK_DEV = 512
TOKENS = 16384
N_SAMPLE = 4
N_FSDP = 8


def draw_resid(key, part):
    first_key, second_key, third_key = jax.random.split(key, 3)
    base = jnp.clip(jax.random.normal(first_key, (TOKENS, D), jnp.float32), -4.0, 4.0)
    row_scale = jnp.exp(jax.random.uniform(second_key, (TOKENS, 1), jnp.float32, -1.2039728, 1.0986123))
    col_scale = jnp.exp(jax.random.uniform(third_key, (1, D), jnp.float32, -1.2039728, 1.0986123))
    return (base * row_scale * col_scale).astype(jnp.bfloat16)


def levels(key, dims, shards, least, largest):
    factor_of, own = 1.0, jax.random.fold_in(key, 6)
    for position, parts in shards:
        steps = jnp.exp(jax.random.uniform(jax.random.fold_in(own, position), (parts,), jnp.float32, least / len(shards), largest / len(shards)))
        factor_of = factor_of * jnp.repeat(steps, dims[position] // parts).reshape([-1 if axis == position else 1 for axis in range(len(dims))])
    return factor_of


def scatter_about(key, dims, scale, most, shards=(), held_as=jnp.bfloat16):
    loudness = levels(key, dims, shards, -0.22, 0.18) if shards else 1.0
    result = jax.random.normal(key, dims, jnp.float32) * scale * loudness
    return jnp.minimum(jnp.maximum(result, -most), most).astype(held_as)


def setup_inputs(seed: int = 0) -> dict:
    seeds = jax.random.split(jax.random.key(seed), 9)
    seed_step = jax.random.randint(seeds[0], (2,), 0, 16777216).astype(jnp.int32)
    attn = scatter_about(seeds[1], (TOKENS, IN), 1.0, 6.0, ((0, 32),))
    resid = draw_resid(jax.random.fold_in(seeds[8], 71), 0)
    cotangent = scatter_about(seeds[3], (TOKENS, D), 1.0, 6.0, ((0, 32),))
    gain = jnp.clip(1.0 + 0.18 * jax.random.normal(seeds[4], (D,), jnp.float32), 0.099609375, 1.8984375).astype(jnp.bfloat16)
    mean = scatter_about(seeds[5], (IN, D), 1.0, 6.0, ((0, 8),), jnp.float32)
    hess = jnp.clip(jnp.exp(math.log(4.0) - 2.7725887 * jax.random.uniform(seeds[6], (IN, D), jnp.float32) ** levels(seeds[6], (IN, D), ((0, 8),), -0.2, 0.2)), 0.25, 4.0)
    momentum = scatter_about(seeds[7], (IN, D), 0.5, 3.0, ((0, 8),), jnp.float32)
    return {"seed_step": seed_step, "attn": attn, "resid": resid, "cotangent": cotangent, "gain": gain, "mean": mean, "hess": hess, "momentum": momentum}


ess_value = 10.0
decay_first = 0.8
decay_second = 0.8
step_size = 0.3
damping = 0.1
norm_eps = 1e-05

def noise_table(seed_step, group_id, row_start, row_count, in_width, width):
    row_index = jnp.arange(row_count, dtype=jnp.int32)[:, None] + row_start
    col_index = jnp.arange(width, dtype=jnp.int32)[None, :]
    mixing = (group_id * in_width + row_index) * width + col_index
    mixing = jnp.bitwise_xor(mixing, seed_step[0])
    mixing = mixing * 668265261 + seed_step[1] * 374761393
    mixing = jnp.bitwise_xor(mixing, jnp.right_shift(mixing, 15) & 131071)
    mixing = mixing * 739982445
    mixing = jnp.bitwise_xor(mixing, jnp.right_shift(mixing, 12) & 1048575)
    mixing = mixing * 695872825
    mixing = jnp.bitwise_xor(mixing, jnp.right_shift(mixing, 15) & 131071)
    first_unif = ((mixing & 4095).astype(jnp.float32) + 0.5) / 4096.0
    second_unif = ((jnp.right_shift(mixing, 12) & 4095).astype(jnp.float32) + 0.5) / 4096.0
    return 2.449489742783178 * (first_unif + second_unif - 1.0)

def reference(seed_step, attn, resid, cotangent, gain, mean, hess, momentum):
    scaling = IN ** (-0.5)
    sigma = 1.0 / jnp.sqrt(ess_value * (hess + damping))
    mean_low = mean.astype(jnp.bfloat16).astype(jnp.float32)
    sigma_low = sigma.astype(jnp.bfloat16).astype(jnp.float32)
    group_rows = TOK_DEV * N_FSDP
    attn_groups = attn.reshape(N_SAMPLE, group_rows, IN)
    resid_groups = resid.reshape(N_SAMPLE, group_rows, D)
    cot_groups = cotangent.reshape(N_SAMPLE, group_rows, D)
    gain_full = gain.astype(jnp.float32)

    def per_group(carry, inputs):
        grad_sum, curv_sum = carry
        group_id, attn_s, resid_s, cot_s = inputs
        epsilon = noise_table(seed_step, group_id, 0, IN, IN, D)
        sampled = (mean_low + sigma_low * epsilon).astype(jnp.bfloat16)
        total = resid_s.astype(jnp.float32) + jnp.dot(attn_s, sampled, preferred_element_type=jnp.float32) * scaling
        inverse = lax.rsqrt(lax.optimization_barrier(jnp.mean(total * total, axis=-1, keepdims=True)) + norm_eps)
        upstream = gain_full * cot_s.astype(jnp.float32)
        back = inverse * upstream - total * inverse ** 3 * lax.optimization_barrier(jnp.mean(total * upstream, axis=-1, keepdims=True))
        back_low = back.astype(jnp.bfloat16)

        def add_part(accum, pair):
            part = (jnp.dot(pair[0].T, pair[1], preferred_element_type=jnp.float32) * scaling).astype(jnp.bfloat16)
            part = lax.optimization_barrier(part)
            return (accum + part.astype(jnp.float32), None)
        grad_s, _ = lax.scan(add_part, jnp.zeros((IN, D), jnp.float32), (attn_s.reshape(N_FSDP, TOK_DEV, IN), back_low.reshape(N_FSDP, TOK_DEV, D)))
        return ((grad_sum + grad_s, curv_sum + grad_s * epsilon / sigma), None)
    start = (jnp.zeros((IN, D), jnp.float32), jnp.zeros((IN, D), jnp.float32))
    (grad_sum, curv_sum), _ = lax.scan(per_group, start, (jnp.arange(N_SAMPLE, dtype=jnp.int32), attn_groups, resid_groups, cot_groups))
    grad_mean = grad_sum / N_SAMPLE
    hess_est = curv_sum / N_SAMPLE
    new_momentum = decay_first * momentum + (1.0 - decay_first) * grad_mean
    new_hess = decay_second * hess + (1.0 - decay_second) * hess_est + 0.5 * (1.0 - decay_second) ** 2 * (hess - hess_est) ** 2 / (hess + damping)
    new_mean = mean - step_size * (new_momentum + damping * mean) / (new_hess + damping)
    return (new_mean, new_hess, new_momentum)
```

```python
import jax
import jax.numpy as jnp
from jax import lax
from jax.experimental.layout import Layout, with_layout_constraint
from jax.sharding import PartitionSpec as P

ess_value = 10.0
decay_first = 0.8
decay_second = 0.8
step_size = 0.3
damping = 0.1
norm_eps = 1e-05


def noise_table(seed_step, group_id, row_start, row_count, in_width, width, col_start, col_count):
    row_index = jnp.arange(row_count, dtype=jnp.int32)[:, None] + row_start
    col_index = jnp.arange(col_count, dtype=jnp.int32)[None, :] + col_start
    mixing = (group_id * in_width + row_index) * width + col_index
    mixing = jnp.bitwise_xor(mixing, seed_step[0])
    mixing = mixing * 668265261 + seed_step[1] * 374761393
    mixing = jnp.bitwise_xor(mixing, jnp.right_shift(mixing, 15) & 131071)
    mixing = mixing * 739982445
    mixing = jnp.bitwise_xor(mixing, jnp.right_shift(mixing, 12) & 1048575)
    mixing = mixing * 695872825
    mixing = jnp.bitwise_xor(mixing, jnp.right_shift(mixing, 15) & 131071)
    first_unif = ((mixing & 4095).astype(jnp.float32) + 0.5) / 4096.0
    second_unif = ((jnp.right_shift(mixing, 12) & 4095).astype(jnp.float32) + 0.5) / 4096.0
    return 2.449489742783178 * (first_unif + second_unif - 1.0)


def ivon_update(mean, hess, momentum, grad_sum, curv_sum, groups):
    grad_mean = grad_sum / groups
    hess_est = curv_sum / groups
    new_momentum = decay_first * momentum + (1.0 - decay_first) * grad_mean
    new_hess = (
        decay_second * hess
        + (1.0 - decay_second) * hess_est
        + 0.5 * (1.0 - decay_second) ** 2 * (hess - hess_est) ** 2 / (hess + damping)
    )
    new_mean = mean - step_size * (new_momentum + damping * mean) / (new_hess + damping)
    return (new_mean, new_hess, new_momentum)


def row_major(value):
    return with_layout_constraint(value, Layout(major_to_minor=(0, 1)))


CHUNKS = 4


def per_device(seed_step, attn, resid, cotangent, gain, mean, hess, momentum):
    own_rows = mean.shape[0]
    width = mean.shape[1]
    in_width = attn.shape[1]
    scaling = in_width ** (-0.5)
    groups = lax.axis_size("sample")
    group_id = lax.axis_index("sample")
    shard_id = lax.axis_index("fsdp")
    part = width // CHUNKS
    cuts = [slice(c * part, (c + 1) * part) for c in range(CHUNKS)]
    epsilons, gathered = [], []
    for c, cut in enumerate(cuts):
        sigma = 1.0 / jnp.sqrt(ess_value * (hess[:, cut] + damping))
        epsilon = noise_table(
            seed_step, group_id, shard_id * own_rows, own_rows, in_width, width, c * part, part
        )
        sampled = (
            mean[:, cut].astype(jnp.bfloat16).astype(jnp.float32)
            + sigma.astype(jnp.bfloat16).astype(jnp.float32) * epsilon
        ).astype(jnp.bfloat16)
        epsilons.append(epsilon / sigma)
        gathered.append(lax.all_gather(row_major(sampled), "fsdp", axis=0, tiled=True))
    totals = []
    square = jnp.zeros((attn.shape[0], 1), jnp.float32)
    cross = jnp.zeros((attn.shape[0], 1), jnp.float32)
    for c, cut in enumerate(cuts):
        product = row_major(
            jnp.dot(attn, row_major(gathered[c]), preferred_element_type=jnp.float32)
        )
        total = resid[:, cut].astype(jnp.float32) + product * scaling
        upstream = gain[cut].astype(jnp.float32)[None, :] * cotangent[:, cut].astype(jnp.float32)
        square = square + jnp.sum(total * total, axis=-1, keepdims=True)
        cross = cross + jnp.sum(total * upstream, axis=-1, keepdims=True)
        totals.append(total)
    inverse = lax.rsqrt(square / width + norm_eps)
    slope = inverse**3 * (cross / width)
    sums = []
    for c, cut in enumerate(cuts):
        upstream = gain[cut].astype(jnp.float32)[None, :] * cotangent[:, cut].astype(jnp.float32)
        back_low = (inverse * upstream - totals[c] * slope).astype(jnp.bfloat16)
        grad = lax.psum_scatter(
            row_major(
                (
                    lax.dot_general(
                        attn,
                        row_major(back_low),
                        (((0,), (0,)), ((), ())),
                        preferred_element_type=jnp.float32,
                    )
                    * scaling
                ).astype(jnp.bfloat16)
            ),
            "fsdp",
            scatter_dimension=0,
            tiled=True,
        )
        if sums:
            grad, sums[-1] = lax.optimization_barrier((grad, sums[-1]))
        grad = row_major(grad)
        curvature = (grad.astype(jnp.float32) * epsilons[c]).astype(jnp.bfloat16)
        sums.append(lax.psum((grad, row_major(curvature)), "sample"))
    grad_sum = jnp.concatenate([s[0] for s in sums], axis=1).astype(jnp.float32)
    curv_sum = jnp.concatenate([s[1] for s in sums], axis=1).astype(jnp.float32)
    return ivon_update(mean, hess, momentum, grad_sum, curv_sum, groups)


def solution(mesh):
    placed = (
        P(),
        P(("sample", "fsdp"), None),
        P(("sample", "fsdp"), None),
        P(("sample", "fsdp"), None),
        P(),
        P("fsdp", None),
        P("fsdp", None),
        P("fsdp", None),
    )
    return jax.shard_map(
        per_device,
        mesh=mesh,
        in_specs=placed,
        out_specs=(P("fsdp", None), P("fsdp", None), P("fsdp", None)),
        check_vma=False,
    )
```

```python
import functools

import jax
import jax.numpy as jnp
from jax import lax
from jax.experimental import pallas as pl
from jax.experimental.pallas import tpu as pltpu
from jax.sharding import PartitionSpec as P

ess_value = 10.0
decay_first = 0.8
decay_second = 0.8
step_size = 0.3
damping = 0.1
norm_eps = 1e-05


def noise_table(seed_step, group_id, row_start, row_count, in_width, width):
    row_index = jnp.arange(row_count, dtype=jnp.int32)[:, None] + row_start
    col_index = jnp.arange(width, dtype=jnp.int32)[None, :]
    mixing = (group_id * in_width + row_index) * width + col_index
    mixing = jnp.bitwise_xor(mixing, seed_step[0])
    mixing = mixing * 668265261 + seed_step[1] * 374761393
    mixing = jnp.bitwise_xor(mixing, jnp.right_shift(mixing, 15) & 131071)
    mixing = mixing * 739982445
    mixing = jnp.bitwise_xor(mixing, jnp.right_shift(mixing, 12) & 1048575)
    mixing = mixing * 695872825
    mixing = jnp.bitwise_xor(mixing, jnp.right_shift(mixing, 15) & 131071)
    first_unif = ((mixing & 4095).astype(jnp.float32) + 0.5) / 4096.0
    second_unif = ((jnp.right_shift(mixing, 12) & 4095).astype(jnp.float32) + 0.5) / 4096.0
    return 2.449489742783178 * (first_unif + second_unif - 1.0)


def ivon_update(mean, hess, momentum, grad_sum, curv_sum, groups):
    grad_mean = grad_sum / groups
    hess_est = curv_sum / groups
    new_momentum = decay_first * momentum + (1.0 - decay_first) * grad_mean
    new_hess = (
        decay_second * hess
        + (1.0 - decay_second) * hess_est
        + 0.5 * (1.0 - decay_second) ** 2 * (hess - hess_est) ** 2 / (hess + damping)
    )
    new_mean = mean - step_size * (new_momentum + damping * mean) / (new_hess + damping)
    return (new_mean, new_hess, new_momentum)


MESH = pl.DeviceIdType.MESH
PIECES = 4


def exchange_kernel(
    line, groups, scaling,
    attn, attn_t, gain, sampled, resid, cotangent, out,
    weights, back, total, paired, chained, ready,
    local_sem, weight_recv, up_send, down_send, core_send,
    pair_send, pair_recv, chain_send, chain_recv, group_send, group_recv,
):
    group = lax.axis_index("sample")
    shard = lax.axis_index("fsdp")
    place = lax.div(shard, 2)
    core = lax.rem(shard, 2)
    twin = place * 2 + 1 - core
    rows, width = sampled.shape
    tokens = attn.shape[0]
    part = width // PIECES
    last = line - 1

    take_resid = pltpu.make_async_copy(resid, back, local_sem.at[0])
    take_resid.start()
    take_own = pltpu.make_async_copy(sampled, weights.at[shard], local_sem.at[1])
    take_own.start()

    barrier = pltpu.get_barrier_semaphore()
    above = lax.rem(place + 1, line) * 2 + core
    below = lax.rem(place + last, line) * 2 + core
    for other in (twin, above, below):
        pl.semaphore_signal(barrier, inc=1, device_id={"fsdp": other}, device_id_type=MESH)
    for step in range(1, groups):
        pl.semaphore_signal(
            barrier, inc=1, device_id={"sample": lax.rem(group + step, groups)}, device_id_type=MESH
        )
    pl.semaphore_wait(barrier, groups + 2)
    take_own.wait()

    def weight_copy(slot, send, other):
        return pltpu.make_async_remote_copy(
            src_ref=weights.at[slot],
            dst_ref=weights.at[slot],
            send_sem=send,
            recv_sem=weight_recv.at[slot],
            device_id={"fsdp": other},
            device_id_type=MESH,
        )

    def wait_weight(slot):
        weight_copy(slot, core_send.at[0], twin).wait_recv()

    def pass_on(slot, up, down):
        if up is not None:
            @pl.when(place < last)
            def _():
                weight_copy(slot, up_send.at[up], above).start()
        if down is not None:
            @pl.when(place > 0)
            def _():
                weight_copy(slot, down_send.at[down], below).start()
        weight_copy(slot, core_send.at[lax.div(slot, 2)], twin).start()

    pass_on(shard, 0, 0)

    take_resid.wait()

    def widen(r, carry):
        sl = pl.ds(pl.multiple_of(r * 32, 32), 32)
        total[sl, :] = back[sl, :].astype(jnp.float32) * (1.0 / scaling)
        return carry

    lax.fori_loop(0, tokens // 32, widen, 0)
    take_cot = pltpu.make_async_copy(cotangent, back, local_sem.at[0])
    take_cot.start()

    def multiply(slot):
        lhs = attn[:, pl.ds(pl.multiple_of(slot * rows, rows), rows)]

        def columns(j, carry):
            sl = pl.ds(pl.multiple_of(j * 512, 512), 512)
            total[:, sl] += jnp.dot(lhs, weights[slot, :, sl], preferred_element_type=jnp.float32)
            return carry

        lax.fori_loop(0, width // 512, columns, 0)

    def multiply_all(slots):
        def one(i, carry):
            slot = slots[-1][0]
            for k in range(len(slots) - 1):
                slot = jnp.where(i == k, slots[k][0], slot)
            wanted = slots[-1][1]
            for k in range(len(slots) - 1):
                wanted = jnp.where(i == k, slots[k][1], wanted)
            from_twin = lax.rem(slot, 2) != core

            @pl.when(wanted)
            def _():
                @pl.when(from_twin)
                def _():
                    wait_weight(slot)
                multiply(slot)
            return carry

        lax.fori_loop(0, len(slots), one, 0)

    always = place >= 0
    multiply_all([(shard, always), (twin, always)])

    def gather_step(t, carry):
        low = place - 1 - t
        high = place + 1 + t
        low_slot = jnp.maximum(low, 0) * 2 + core
        high_slot = jnp.minimum(high, last) * 2 + core

        @pl.when(low >= 0)
        def _():
            wait_weight(low_slot)
            pass_on(low_slot, t + 1, None)

        @pl.when(high <= last)
        def _():
            wait_weight(high_slot)
            pass_on(high_slot, None, t + 1)

        multiply_all([
            (low_slot, low >= 0),
            (high_slot, high <= last),
            (low_slot + 1 - 2 * core, low >= 0),
            (high_slot + 1 - 2 * core, high <= last),
        ])
        return carry

    lax.fori_loop(0, last, gather_step, 0)

    def drain_weights(t, carry):
        @pl.when((place < last) & (place - t >= 0))
        def _():
            weight_copy(shard, up_send.at[t], above).wait_send()

        @pl.when((place > 0) & (place + t <= last))
        def _():
            weight_copy(shard, down_send.at[t], below).wait_send()

        weight_copy(shard, core_send.at[t], twin).wait_send()
        return carry

    lax.fori_loop(0, line, drain_weights, 0)

    take_cot.wait()
    span = 512

    def normalise(r, carry):
        sl = pl.ds(pl.multiple_of(r * 16, 16), 16)
        square = jnp.zeros((16, span), jnp.float32)
        cross = jnp.zeros((16, span), jnp.float32)
        for c in range(width // span):
            cs = pl.ds(c * span, span)
            value = total[sl, cs] * scaling
            upstream = gain[:, cs] * back[sl, cs].astype(jnp.float32)
            square = square + value * value
            cross = cross + value * upstream
        inverse = lax.rsqrt(jnp.sum(square, axis=-1, keepdims=True) * (1.0 / width) + norm_eps)
        slope = inverse * inverse * inverse * (
            jnp.sum(cross, axis=-1, keepdims=True) * (1.0 / width)
        )
        for c in range(width // span):
            cs = pl.ds(c * span, span)
            value = total[sl, cs] * scaling
            upstream = gain[:, cs] * back[sl, cs].astype(jnp.float32)
            back[sl, cs] = (inverse * upstream - value * slope).astype(jnp.bfloat16)
        return carry

    lax.fori_loop(0, tokens // 16, normalise, 0)

    def partial(block, piece):
        lhs = attn_t[pl.ds(pl.multiple_of(block * rows, rows), rows), :]
        rhs = back[:, pl.ds(pl.multiple_of(piece * part, part), part)]
        return jnp.dot(lhs, rhs, preferred_element_type=jnp.float32) * scaling

    def pair_copy(goal, piece):
        return pltpu.make_async_remote_copy(
            src_ref=weights.at[goal, :, pl.ds(pl.multiple_of(piece * part, part), part)],
            dst_ref=paired.at[goal, piece],
            send_sem=pair_send.at[goal, piece],
            recv_sem=pair_recv.at[goal, piece],
            device_id={"fsdp": twin},
            device_id_type=MESH,
        )

    def give_twin(i, piece):
        goal = i
        weights[goal, :, pl.ds(pl.multiple_of(piece * part, part), part)] = partial(
            goal * 2 + 1 - core, piece
        ).astype(jnp.bfloat16)
        pair_copy(goal, piece).start()
        return piece

    def chain_copy(goal, slot, piece, other):
        return pltpu.make_async_remote_copy(
            src_ref=chained.at[goal, piece],
            dst_ref=chained.at[slot, piece],
            send_sem=chain_send.at[goal, piece],
            recv_sem=chain_recv.at[slot, piece],
            device_id={"fsdp": other},
            device_id_type=MESH,
        )

    def own_term(goal, piece):
        pair_copy(goal, piece).wait_recv()
        return partial(goal * 2 + core, piece) + paired[goal, piece].astype(jnp.float32)

    def forward(goal, piece, first, slot, other):
        @pl.when(first)
        def _():
            chained[goal, piece] = own_term(goal, piece).astype(jnp.bfloat16)

        @pl.when(jnp.logical_not(first))
        def _():
            chain_copy(goal, goal, piece, other).wait_recv()
            chained[goal, piece] = (
                own_term(goal, piece) + chained[goal, piece].astype(jnp.float32)
            ).astype(jnp.bfloat16)

        chain_copy(goal, slot, piece, other).start()

    def group_copy(piece, step):
        cs = pl.ds(pl.multiple_of(piece * part, part), part)
        return pltpu.make_async_remote_copy(
            src_ref=ready.at[piece],
            dst_ref=out.at[group, :, cs],
            send_sem=group_send.at[step, piece],
            recv_sem=group_recv.at[group, piece],
            device_id={"sample": lax.rem(group + step, groups)},
            device_id_type=MESH,
        )

    def keep_copy(piece):
        cs = pl.ds(pl.multiple_of(piece * part, part), part)
        return pltpu.make_async_copy(
            ready.at[piece], out.at[group, :, cs], group_send.at[0, piece]
        )

    @pl.when(place == 0)
    def _():
        chained[0] = jnp.zeros(chained.shape[1:], chained.dtype)

    @pl.when(place == last)
    def _():
        chained[line] = jnp.zeros(chained.shape[1:], chained.dtype)

    lax.fori_loop(0, line, give_twin, 0)

    def reduce_step(step, carry):
        up_at = step - place
        up_piece = lax.div(jnp.maximum(up_at, 0), last)
        up_goal = last - lax.rem(jnp.maximum(up_at, 0), last)

        @pl.when((up_at >= 0) & (up_piece < PIECES) & (up_goal > place))
        def _():
            forward(up_goal, up_piece, place == 0, up_goal, above)

        down_at = step - (last - place)
        down_piece = lax.div(jnp.maximum(down_at, 0), last)
        down_goal = lax.rem(jnp.maximum(down_at, 0), last)

        @pl.when((down_at >= 0) & (down_piece < PIECES) & (down_goal < place))
        def _():
            slot = jnp.where(down_goal == place - 1, line, down_goal)
            forward(down_goal, down_piece, place == last, slot, below)

        turn = lax.div(step, last)

        @pl.when((lax.rem(step, last) == 0) & (turn < PIECES - 1))
        def _():
            lax.fori_loop(0, line, give_twin, turn + 1)

        @pl.when((lax.rem(step, last) == 0) & (turn >= 1))
        def _():
            piece = turn - 1

            @pl.when(place > 0)
            def _():
                chain_copy(place, place, piece, below).wait_recv()

            @pl.when(place < last)
            def _():
                chain_copy(place, line, piece, above).wait_recv()

            ready[piece] = (
                own_term(place, piece)
                + chained[place, piece].astype(jnp.float32)
                + chained[line, piece].astype(jnp.float32)
            ).astype(jnp.bfloat16)
            for k in range(1, groups):
                group_copy(piece, k).start()
            keep_copy(piece).start()
        return carry

    lax.fori_loop(0, PIECES * last + 1, reduce_step, 0)

    def finish(piece, carry):
        def goals(goal, inner):
            pair_copy(goal, piece).wait_send()

            @pl.when(goal != place)
            def _():
                chain_copy(goal, goal, piece, above).wait_send()
            return inner

        lax.fori_loop(0, line, goals, 0)
        keep_copy(piece).wait()
        for k in range(1, groups):
            group_copy(piece, k).wait_send()
            source = lax.rem(group + k, groups)
            cs = pl.ds(pl.multiple_of(piece * part, part), part)
            pltpu.make_async_remote_copy(
                src_ref=ready.at[piece],
                dst_ref=out.at[source, :, cs],
                send_sem=group_send.at[k, piece],
                recv_sem=group_recv.at[source, piece],
                device_id={"sample": source},
                device_id_type=MESH,
            ).wait_recv()
        return carry

    lax.fori_loop(0, PIECES, finish, 0)


def exchange(attn, resid, cotangent, gain, sampled, scaling):
    line = lax.axis_size("fsdp") // 2
    groups = lax.axis_size("sample")
    tokens, width = resid.shape
    rows = sampled.shape[0]
    part = width // PIECES
    vmem = pl.BlockSpec(memory_space=pltpu.VMEM)
    hbm = pl.BlockSpec(memory_space=pl.ANY)
    dma = pltpu.SemaphoreType.DMA
    return pl.pallas_call(
        functools.partial(exchange_kernel, line, groups, scaling),
        out_shape=jax.ShapeDtypeStruct((groups, rows, width), jnp.bfloat16),
        in_specs=[vmem, vmem, vmem, hbm, hbm, hbm],
        out_specs=hbm,
        scratch_shapes=[
            pltpu.VMEM((2 * line, rows, width), jnp.bfloat16),
            pltpu.VMEM((tokens, width), jnp.bfloat16),
            pltpu.VMEM((tokens, width), jnp.float32),
            pltpu.VMEM((line, PIECES, rows, part), jnp.bfloat16),
            pltpu.VMEM((line + 1, PIECES, rows, part), jnp.bfloat16),
            pltpu.VMEM((PIECES, rows, part), jnp.bfloat16),
            dma((2,)),
            dma((2 * line,)),
            dma((line,)),
            dma((line,)),
            dma((line,)),
            dma((line, PIECES)),
            dma((line, PIECES)),
            dma((line, PIECES)),
            dma((line + 1, PIECES)),
            dma((groups, PIECES)),
            dma((groups, PIECES)),
        ],
        compiler_params=pltpu.CompilerParams(
            collective_id=0, has_side_effects=True, vmem_limit_bytes=60 * 2**20
        ),
    )(attn, attn.T, gain.astype(jnp.float32)[None, :], sampled, resid, cotangent)


def per_device(seed_step, attn, resid, cotangent, gain, mean, hess, momentum):
    own_rows = mean.shape[0]
    width = mean.shape[1]
    in_width = attn.shape[1]
    scaling = in_width ** (-0.5)
    groups = lax.axis_size("sample")
    group_id = lax.axis_index("sample")
    row_start = lax.axis_index("fsdp") * own_rows
    sigma = 1.0 / jnp.sqrt(ess_value * (hess + damping))
    epsilon = noise_table(seed_step, group_id, row_start, own_rows, in_width, width)
    sampled = (
        mean.astype(jnp.bfloat16).astype(jnp.float32)
        + sigma.astype(jnp.bfloat16).astype(jnp.float32) * epsilon
    ).astype(jnp.bfloat16)
    grads = exchange(attn, resid, cotangent, gain, sampled, scaling)
    grad_sum = jnp.zeros((own_rows, width), jnp.float32)
    curv_sum = jnp.zeros((own_rows, width), jnp.float32)
    for g in range(groups):
        grad = grads[g].astype(jnp.float32)
        noise = noise_table(seed_step, g, row_start, own_rows, in_width, width)
        grad_sum = grad_sum + grad
        curv_sum = curv_sum + grad * noise
    return ivon_update(mean, hess, momentum, grad_sum, curv_sum / sigma, groups)


def solution(mesh):
    placed = (
        P(),
        P(("sample", "fsdp"), None),
        P(("sample", "fsdp"), None),
        P(("sample", "fsdp"), None),
        P(),
        P("fsdp", None),
        P("fsdp", None),
        P("fsdp", None),
    )
    return jax.shard_map(
        per_device,
        mesh=mesh,
        in_specs=placed,
        out_specs=(P("fsdp", None), P("fsdp", None), P("fsdp", None)),
        check_vma=False,
    )
```

```python
import functools

import jax
import jax.numpy as jnp
from jax import lax
from jax.experimental import pallas as pl
from jax.experimental.pallas import tpu as pltpu
from jax.sharding import PartitionSpec as P

ess_value = 10.0
decay_first = 0.8
decay_second = 0.8
step_size = 0.3
damping = 0.1
norm_eps = 1e-05


noise_scale = 2.449489742783178


def noise_count(mixing, seed, key):
    mixing = jnp.bitwise_xor(mixing, seed)
    mixing = mixing * 668265261 + key
    mixing = jnp.bitwise_xor(mixing, jnp.right_shift(mixing, 15) & 131071)
    mixing = mixing * 739982445
    mixing = jnp.bitwise_xor(mixing, jnp.right_shift(mixing, 12) & 1048575)
    mixing = mixing * 695872825
    mixing = jnp.bitwise_xor(mixing, jnp.right_shift(mixing, 15) & 131071)
    return (mixing & 4095) + (jnp.right_shift(mixing, 12) & 4095)


def noise_table(seed_step, group_id, row_start, row_count, in_width, width):
    row_index = jnp.arange(row_count, dtype=jnp.int32)[:, None] + row_start
    col_index = jnp.arange(width, dtype=jnp.int32)[None, :]
    mixing = (group_id * in_width + row_index) * width + col_index
    count = noise_count(mixing, seed_step[0], seed_step[1] * 374761393)
    return noise_scale * ((count.astype(jnp.float32) + 1.0) / 4096.0 - 1.0)


def ivon_update(mean, hess, momentum, grad_sum, curv_sum, groups):
    grad_mean = grad_sum / groups
    hess_est = curv_sum / groups
    new_momentum = decay_first * momentum + (1.0 - decay_first) * grad_mean
    new_hess = (
        decay_second * hess
        + (1.0 - decay_second) * hess_est
        + 0.5 * (1.0 - decay_second) ** 2 * (hess - hess_est) ** 2 / (hess + damping)
    )
    new_mean = mean - step_size * (new_momentum + damping * mean) / (new_hess + damping)
    return (new_mean, new_hess, new_momentum)


MESH = pl.DeviceIdType.MESH
PIECES = 8
SLICES = 4
SPAN = 512


def exchange_kernel(
    line, groups, scaling,
    seed_step, attn, attn_t, gain, sampled, resid, cotangent, out, noise_out,
    weights, back, total, paired, chained, ready, stage,
    noise_sem, local_sem, weight_recv, up_send, down_send, core_send,
    pair_send, pair_recv, chain_send, chain_recv, group_send, group_recv,
):
    group = lax.axis_index("sample")
    shard = lax.axis_index("fsdp")
    place = lax.div(shard, 2)
    core = lax.rem(shard, 2)
    twin = place * 2 + 1 - core
    rows, width = sampled.shape
    tokens, in_width = attn.shape
    part = width // PIECES
    last = line - 1

    take_resid = pltpu.make_async_copy(resid, back, local_sem.at[0])
    take_resid.start()
    take_own = pltpu.make_async_copy(sampled, weights.at[shard], local_sem.at[1])
    take_own.start()

    barrier = pltpu.get_barrier_semaphore()
    above = lax.rem(place + 1, line) * 2 + core
    below = lax.rem(place + last, line) * 2 + core
    for other in (twin, above, below):
        pl.semaphore_signal(barrier, inc=1, device_id={"fsdp": other}, device_id_type=MESH)
    for step in range(1, groups):
        pl.semaphore_signal(
            barrier, inc=1, device_id={"sample": lax.rem(group + step, groups)}, device_id_type=MESH
        )
    pl.semaphore_wait(barrier, groups + 2)
    take_own.wait()

    piece_width = width // SLICES

    def weight_copy(slot, h, send, other):
        cs = pl.ds(pl.multiple_of(h * piece_width, piece_width), piece_width)
        return pltpu.make_async_remote_copy(
            src_ref=weights.at[slot, :, cs],
            dst_ref=weights.at[slot, :, cs],
            send_sem=send,
            recv_sem=weight_recv.at[slot, h],
            device_id={"fsdp": other},
            device_id_type=MESH,
        )

    def wait_weight(slot, h):
        weight_copy(slot, h, core_send.at[0, h], twin).wait_recv()

    def pass_on(slot, h, up, down):
        if up is not None:
            @pl.when(place < last)
            def _():
                weight_copy(slot, h, up_send.at[up, h], above).start()
        if down is not None:
            @pl.when(place > 0)
            def _():
                weight_copy(slot, h, down_send.at[down, h], below).start()
        weight_copy(slot, h, core_send.at[lax.div(slot, 2), h], twin).start()

    def pass_own(h, carry):
        pass_on(shard, h, 0, 0)
        return carry

    lax.fori_loop(0, SLICES, pass_own, 0)

    units = groups * (width // SPAN)

    def noise_copy(u):
        per = width // SPAN
        cs = pl.ds(pl.multiple_of(lax.rem(u, per) * SPAN, SPAN), SPAN)
        return pltpu.make_async_copy(
            stage.at[lax.rem(u, 2)],
            noise_out.at[lax.div(u, per), :, cs],
            noise_sem.at[lax.rem(u, 2)],
        )

    seed = seed_step[0]
    key = seed_step[1] * 374761393

    def noise_unit(u, carry):
        per = width // SPAN
        slot = lax.rem(u, 2)

        @pl.when(u >= 2)
        def _():
            noise_copy(u - 2).wait()

        base = (lax.div(u, per) * in_width + shard * rows) * width + lax.rem(u, per) * SPAN

        def some_rows(r, inner):
            index = (
                lax.broadcasted_iota(jnp.int32, (32, SPAN), 0) * width
                + lax.broadcasted_iota(jnp.int32, (32, SPAN), 1)
                + (base + r * 32 * width)
            )
            count = noise_count(index, seed, key)
            stage[slot, pl.ds(pl.multiple_of(r * 32, 32), 32), :] = count.astype(jnp.int16)
            return inner

        lax.fori_loop(0, rows // 32, some_rows, 0)
        noise_copy(u).start()
        return carry

    take_resid.wait()

    def widen(r, carry):
        sl = pl.ds(pl.multiple_of(r * 32, 32), 32)
        total[sl, :] = back[sl, :].astype(jnp.float32) * (1.0 / scaling)
        return carry

    lax.fori_loop(0, tokens // 32, widen, 0)
    take_cot = pltpu.make_async_copy(cotangent, back, local_sem.at[0])
    take_cot.start()

    def multiply(slot, h):
        lhs = attn[:, pl.ds(pl.multiple_of(slot * rows, rows), rows)]

        def columns(j, carry):
            sl = pl.ds(pl.multiple_of(h * piece_width + j * 512, 512), 512)
            total[:, sl] += jnp.dot(lhs, weights[slot, :, sl], preferred_element_type=jnp.float32)
            return carry

        lax.fori_loop(0, piece_width // 512, columns, 0)

    def multiply_all(slots, h):
        def one(i, carry):
            slot = slots[-1][0]
            for k in range(len(slots) - 1):
                slot = jnp.where(i == k, slots[k][0], slot)
            wanted = slots[-1][1]
            for k in range(len(slots) - 1):
                wanted = jnp.where(i == k, slots[k][1], wanted)
            from_twin = lax.rem(slot, 2) != core

            @pl.when(wanted)
            def _():
                @pl.when(from_twin)
                def _():
                    wait_weight(slot, h)
                multiply(slot, h)
            return carry

        lax.fori_loop(0, len(slots), one, 0)

    always = place >= 0

    def multiply_own(h, carry):
        multiply_all([(shard, always), (twin, always)], h)
        return carry

    def gather_step(i, carry):
        t = lax.div(i, SLICES)
        h = lax.rem(i, SLICES)
        low = place - 1 - t
        high = place + 1 + t
        low_slot = jnp.maximum(low, 0) * 2 + core
        high_slot = jnp.minimum(high, last) * 2 + core

        @pl.when(low >= 0)
        def _():
            wait_weight(low_slot, h)
            pass_on(low_slot, h, t + 1, None)

        @pl.when(high <= last)
        def _():
            wait_weight(high_slot, h)
            pass_on(high_slot, h, None, t + 1)

        @pl.when(i == 0)
        def _():
            lax.fori_loop(0, SLICES, multiply_own, 0)

        steps = last * SLICES - 1
        lax.fori_loop(
            lax.div(units * jnp.minimum(i, steps), steps),
            lax.div(units * jnp.minimum(i + 1, steps), steps),
            noise_unit,
            0,
        )
        multiply_all([
            (low_slot, low >= 0),
            (high_slot, high <= last),
            (low_slot + 1 - 2 * core, low >= 0),
            (high_slot + 1 - 2 * core, high <= last),
        ], h)
        return carry

    lax.fori_loop(0, last * SLICES, gather_step, 0)
    noise_copy(units - 2).wait()
    noise_copy(units - 1).wait()

    def drain_weights(i, carry):
        t = lax.div(i, SLICES)
        h = lax.rem(i, SLICES)

        @pl.when((place < last) & (place - t >= 0))
        def _():
            weight_copy(shard, h, up_send.at[t, h], above).wait_send()

        @pl.when((place > 0) & (place + t <= last))
        def _():
            weight_copy(shard, h, down_send.at[t, h], below).wait_send()

        weight_copy(shard, h, core_send.at[t, h], twin).wait_send()
        return carry

    lax.fori_loop(0, line * SLICES, drain_weights, 0)

    take_cot.wait()
    span = 512

    def normalise(r, carry):
        sl = pl.ds(pl.multiple_of(r * 16, 16), 16)
        square = jnp.zeros((16, span), jnp.float32)
        cross = jnp.zeros((16, span), jnp.float32)
        for c in range(width // span):
            cs = pl.ds(c * span, span)
            value = total[sl, cs] * scaling
            upstream = gain[:, cs] * back[sl, cs].astype(jnp.float32)
            square = square + value * value
            cross = cross + value * upstream
        inverse = lax.rsqrt(jnp.sum(square, axis=-1, keepdims=True) * (1.0 / width) + norm_eps)
        slope = inverse * inverse * inverse * (
            jnp.sum(cross, axis=-1, keepdims=True) * (1.0 / width)
        )
        for c in range(width // span):
            cs = pl.ds(c * span, span)
            value = total[sl, cs] * scaling
            upstream = gain[:, cs] * back[sl, cs].astype(jnp.float32)
            back[sl, cs] = (inverse * upstream - value * slope).astype(jnp.bfloat16)
        return carry

    lax.fori_loop(0, tokens // 16, normalise, 0)

    def partial(block, piece):
        lhs = attn_t[pl.ds(pl.multiple_of(block * rows, rows), rows), :]
        rhs = back[:, pl.ds(pl.multiple_of(piece * part, part), part)]
        return jnp.dot(lhs, rhs, preferred_element_type=jnp.float32) * scaling

    def pair_copy(goal, piece):
        return pltpu.make_async_remote_copy(
            src_ref=weights.at[goal, :, pl.ds(pl.multiple_of(piece * part, part), part)],
            dst_ref=paired.at[goal, piece],
            send_sem=pair_send.at[goal, piece],
            recv_sem=pair_recv.at[goal, piece],
            device_id={"fsdp": twin},
            device_id_type=MESH,
        )

    def give_twin(i, piece):
        goal = i
        weights[goal, :, pl.ds(pl.multiple_of(piece * part, part), part)] = partial(
            goal * 2 + 1 - core, piece
        ).astype(jnp.bfloat16)
        pair_copy(goal, piece).start()
        return piece

    def chain_copy(goal, slot, piece, other):
        return pltpu.make_async_remote_copy(
            src_ref=chained.at[goal, piece],
            dst_ref=chained.at[slot, piece],
            send_sem=chain_send.at[goal, piece],
            recv_sem=chain_recv.at[slot, piece],
            device_id={"fsdp": other},
            device_id_type=MESH,
        )

    def own_term(goal, piece):
        pair_copy(goal, piece).wait_recv()
        return partial(goal * 2 + core, piece) + paired[goal, piece].astype(jnp.float32)

    def forward(goal, piece, first, slot, other):
        @pl.when(first)
        def _():
            chained[goal, piece] = own_term(goal, piece).astype(jnp.bfloat16)

        @pl.when(jnp.logical_not(first))
        def _():
            chain_copy(goal, goal, piece, other).wait_recv()
            chained[goal, piece] = (
                own_term(goal, piece) + chained[goal, piece].astype(jnp.float32)
            ).astype(jnp.bfloat16)

        chain_copy(goal, slot, piece, other).start()

    def group_copy(piece, step):
        cs = pl.ds(pl.multiple_of(piece * part, part), part)
        return pltpu.make_async_remote_copy(
            src_ref=ready.at[piece],
            dst_ref=out.at[group, :, cs],
            send_sem=group_send.at[step, piece],
            recv_sem=group_recv.at[group, piece],
            device_id={"sample": lax.rem(group + step, groups)},
            device_id_type=MESH,
        )

    def keep_copy(piece):
        cs = pl.ds(pl.multiple_of(piece * part, part), part)
        return pltpu.make_async_copy(
            ready.at[piece], out.at[group, :, cs], group_send.at[0, piece]
        )

    @pl.when(place == 0)
    def _():
        chained[0] = jnp.zeros(chained.shape[1:], chained.dtype)

    @pl.when(place == last)
    def _():
        chained[line] = jnp.zeros(chained.shape[1:], chained.dtype)

    lax.fori_loop(0, line, give_twin, 0)

    def reduce_step(step, carry):
        up_at = step - place
        up_piece = lax.div(jnp.maximum(up_at, 0), last)
        up_goal = last - lax.rem(jnp.maximum(up_at, 0), last)

        @pl.when((up_at >= 0) & (up_piece < PIECES) & (up_goal > place))
        def _():
            forward(up_goal, up_piece, place == 0, up_goal, above)

        down_at = step - (last - place)
        down_piece = lax.div(jnp.maximum(down_at, 0), last)
        down_goal = lax.rem(jnp.maximum(down_at, 0), last)

        @pl.when((down_at >= 0) & (down_piece < PIECES) & (down_goal < place))
        def _():
            slot = jnp.where(down_goal == place - 1, line, down_goal)
            forward(down_goal, down_piece, place == last, slot, below)

        turn = lax.div(step, last)

        @pl.when((lax.rem(step, last) == 0) & (turn < PIECES - 1))
        def _():
            lax.fori_loop(0, line, give_twin, turn + 1)

        @pl.when((lax.rem(step, last) == 0) & (turn >= 1))
        def _():
            piece = turn - 1

            @pl.when(place > 0)
            def _():
                chain_copy(place, place, piece, below).wait_recv()

            @pl.when(place < last)
            def _():
                chain_copy(place, line, piece, above).wait_recv()

            ready[piece] = (
                own_term(place, piece)
                + chained[place, piece].astype(jnp.float32)
                + chained[line, piece].astype(jnp.float32)
            ).astype(jnp.bfloat16)
            for k in range(1, groups):
                group_copy(piece, k).start()
            keep_copy(piece).start()
        return carry

    lax.fori_loop(0, PIECES * last + 1, reduce_step, 0)

    def finish(piece, carry):
        def goals(goal, inner):
            pair_copy(goal, piece).wait_send()

            @pl.when(goal != place)
            def _():
                chain_copy(goal, goal, piece, above).wait_send()
            return inner

        lax.fori_loop(0, line, goals, 0)
        keep_copy(piece).wait()
        for k in range(1, groups):
            group_copy(piece, k).wait_send()
            source = lax.rem(group + k, groups)
            cs = pl.ds(pl.multiple_of(piece * part, part), part)
            pltpu.make_async_remote_copy(
                src_ref=ready.at[piece],
                dst_ref=out.at[source, :, cs],
                send_sem=group_send.at[k, piece],
                recv_sem=group_recv.at[source, piece],
                device_id={"sample": source},
                device_id_type=MESH,
            ).wait_recv()
        return carry

    lax.fori_loop(0, PIECES, finish, 0)


def exchange(seed_step, attn, resid, cotangent, gain, sampled, scaling):
    line = lax.axis_size("fsdp") // 2
    groups = lax.axis_size("sample")
    tokens, width = resid.shape
    rows = sampled.shape[0]
    part = width // PIECES
    vmem = pl.BlockSpec(memory_space=pltpu.VMEM)
    hbm = pl.BlockSpec(memory_space=pl.ANY)
    dma = pltpu.SemaphoreType.DMA
    return pl.pallas_call(
        functools.partial(exchange_kernel, line, groups, scaling),
        out_shape=(
            jax.ShapeDtypeStruct((groups, rows, width), jnp.bfloat16),
            jax.ShapeDtypeStruct((groups, rows, width), jnp.int16),
        ),
        in_specs=[pl.BlockSpec(memory_space=pltpu.SMEM), vmem, vmem, vmem, hbm, hbm, hbm],
        out_specs=(hbm, hbm),
        scratch_shapes=[
            pltpu.VMEM((2 * line, rows, width), jnp.bfloat16),
            pltpu.VMEM((tokens, width), jnp.bfloat16),
            pltpu.VMEM((tokens, width), jnp.float32),
            pltpu.VMEM((line, PIECES, rows, part), jnp.bfloat16),
            pltpu.VMEM((line + 1, PIECES, rows, part), jnp.bfloat16),
            pltpu.VMEM((PIECES, rows, part), jnp.bfloat16),
            pltpu.VMEM((2, rows, SPAN), jnp.int16),
            dma((2,)),
            dma((2,)),
            dma((2 * line, SLICES)),
            dma((line, SLICES)),
            dma((line, SLICES)),
            dma((line, SLICES)),
            dma((line, PIECES)),
            dma((line, PIECES)),
            dma((line, PIECES)),
            dma((line + 1, PIECES)),
            dma((groups, PIECES)),
            dma((groups, PIECES)),
        ],
        compiler_params=pltpu.CompilerParams(
            collective_id=0, has_side_effects=True, vmem_limit_bytes=60 * 2**20
        ),
    )(seed_step, attn, attn.T, gain.astype(jnp.float32)[None, :], sampled, resid, cotangent)


def per_device(seed_step, attn, resid, cotangent, gain, mean, hess, momentum):
    own_rows = mean.shape[0]
    width = mean.shape[1]
    in_width = attn.shape[1]
    scaling = in_width ** (-0.5)
    groups = lax.axis_size("sample")
    group_id = lax.axis_index("sample")
    row_start = lax.axis_index("fsdp") * own_rows
    sigma = 1.0 / jnp.sqrt(ess_value * (hess + damping))
    epsilon = noise_table(seed_step, group_id, row_start, own_rows, in_width, width)
    sampled = (
        mean.astype(jnp.bfloat16).astype(jnp.float32)
        + sigma.astype(jnp.bfloat16).astype(jnp.float32) * epsilon
    ).astype(jnp.bfloat16)
    grads, counts = exchange(seed_step, attn, resid, cotangent, gain, sampled, scaling)
    grad_sum = jnp.zeros((own_rows, width), jnp.float32)
    curv_sum = jnp.zeros((own_rows, width), jnp.float32)
    for g in range(groups):
        grad = grads[g].astype(jnp.float32)
        noise = noise_scale * ((counts[g].astype(jnp.float32) + 1.0) / 4096.0 - 1.0)
        grad_sum = grad_sum + grad
        curv_sum = curv_sum + grad * noise
    return ivon_update(mean, hess, momentum, grad_sum, curv_sum / sigma, groups)


def solution(mesh):
    placed = (
        P(),
        P(("sample", "fsdp"), None),
        P(("sample", "fsdp"), None),
        P(("sample", "fsdp"), None),
        P(),
        P("fsdp", None),
        P("fsdp", None),
        P("fsdp", None),
    )
    return jax.shard_map(
        per_device,
        mesh=mesh,
        in_specs=placed,
        out_specs=(P("fsdp", None), P("fsdp", None), P("fsdp", None)),
        check_vma=False,
    )
```

```python
import functools

import jax
import jax.numpy as jnp
from jax import lax
from jax.experimental import pallas as pl
from jax.experimental.pallas import tpu as pltpu
from jax.sharding import PartitionSpec as P

ess_value = 10.0
decay_first = 0.8
decay_second = 0.8
step_size = 0.3
damping = 0.1
norm_eps = 1e-05


noise_scale = 2.449489742783178


def noise_count(mixing, seed, key):
    mixing = jnp.bitwise_xor(mixing, seed)
    mixing = mixing * 668265261 + key
    mixing = jnp.bitwise_xor(mixing, jnp.right_shift(mixing, 15) & 131071)
    mixing = mixing * 739982445
    mixing = jnp.bitwise_xor(mixing, jnp.right_shift(mixing, 12) & 1048575)
    mixing = mixing * 695872825
    mixing = jnp.bitwise_xor(mixing, jnp.right_shift(mixing, 15) & 131071)
    return (mixing & 4095) + (jnp.right_shift(mixing, 12) & 4095)


def noise_table(seed_step, group_id, row_start, row_count, in_width, width):
    row_index = jnp.arange(row_count, dtype=jnp.int32)[:, None] + row_start
    col_index = jnp.arange(width, dtype=jnp.int32)[None, :]
    mixing = (group_id * in_width + row_index) * width + col_index
    count = noise_count(mixing, seed_step[0], seed_step[1] * 374761393)
    return noise_scale * ((count.astype(jnp.float32) + 1.0) / 4096.0 - 1.0)


def ivon_update(mean, hess, momentum, grad_sum, curv_sum, groups):
    grad_mean = grad_sum / groups
    hess_est = curv_sum / groups
    new_momentum = decay_first * momentum + (1.0 - decay_first) * grad_mean
    new_hess = (
        decay_second * hess
        + (1.0 - decay_second) * hess_est
        + 0.5 * (1.0 - decay_second) ** 2 * (hess - hess_est) ** 2 / (hess + damping)
    )
    new_mean = mean - step_size * (new_momentum + damping * mean) / (new_hess + damping)
    return (new_mean, new_hess, new_momentum)


MESH = pl.DeviceIdType.MESH
PIECES = 8
SLICES = 4
SPAN = 512


def exchange_kernel(
    line, groups, scaling,
    seed_step, attn, gain, sampled, resid, cotangent, out, noise_out,
    weights, back, total, paired, chained, ready, stage,
    noise_sem, local_sem, weight_recv, up_send, down_send, core_send,
    pair_send, pair_recv, chain_send, chain_recv, group_send, group_recv,
):
    group = lax.axis_index("sample")
    shard = lax.axis_index("fsdp")
    place = lax.div(shard, 2)
    core = lax.rem(shard, 2)
    twin = place * 2 + 1 - core
    rows, width = sampled.shape
    tokens, in_width = attn.shape
    part = width // PIECES
    last = line - 1

    take_resid = pltpu.make_async_copy(resid, back, local_sem.at[0])
    take_resid.start()
    take_own = pltpu.make_async_copy(sampled, weights.at[shard], local_sem.at[1])
    take_own.start()

    barrier = pltpu.get_barrier_semaphore()
    above = lax.rem(place + 1, line) * 2 + core
    below = lax.rem(place + last, line) * 2 + core
    for other in (twin, above, below):
        pl.semaphore_signal(barrier, inc=1, device_id={"fsdp": other}, device_id_type=MESH)
    for step in range(1, groups):
        pl.semaphore_signal(
            barrier, inc=1, device_id={"sample": lax.rem(group + step, groups)}, device_id_type=MESH
        )
    pl.semaphore_wait(barrier, groups + 2)
    take_own.wait()

    piece_width = width // SLICES

    def weight_copy(slot, h, send, other):
        cs = pl.ds(pl.multiple_of(h * piece_width, piece_width), piece_width)
        return pltpu.make_async_remote_copy(
            src_ref=weights.at[slot, :, cs],
            dst_ref=weights.at[slot, :, cs],
            send_sem=send,
            recv_sem=weight_recv.at[slot, h],
            device_id={"fsdp": other},
            device_id_type=MESH,
        )

    def wait_weight(slot, h):
        weight_copy(slot, h, core_send.at[0, h], twin).wait_recv()

    def pass_on(slot, h, up, down):
        if up is not None:
            @pl.when(place < last)
            def _():
                weight_copy(slot, h, up_send.at[up, h], above).start()
        if down is not None:
            @pl.when(place > 0)
            def _():
                weight_copy(slot, h, down_send.at[down, h], below).start()
        weight_copy(slot, h, core_send.at[lax.div(slot, 2), h], twin).start()

    def pass_own(h, carry):
        pass_on(shard, h, 0, 0)
        return carry

    lax.fori_loop(0, SLICES, pass_own, 0)

    units = groups * (width // SPAN)

    def noise_copy(u):
        per = width // SPAN
        cs = pl.ds(pl.multiple_of(lax.rem(u, per) * SPAN, SPAN), SPAN)
        return pltpu.make_async_copy(
            stage.at[lax.rem(u, 2)],
            noise_out.at[lax.div(u, per), :, cs],
            noise_sem.at[lax.rem(u, 2)],
        )

    seed = seed_step[0]
    key = seed_step[1] * 374761393

    def noise_unit(u, carry):
        per = width // SPAN
        slot = lax.rem(u, 2)

        @pl.when(u >= 2)
        def _():
            noise_copy(u - 2).wait()

        base = (lax.div(u, per) * in_width + shard * rows) * width + lax.rem(u, per) * SPAN

        def some_rows(r, inner):
            index = (
                lax.broadcasted_iota(jnp.int32, (32, SPAN), 0) * width
                + lax.broadcasted_iota(jnp.int32, (32, SPAN), 1)
                + (base + r * 32 * width)
            )
            count = noise_count(index, seed, key)
            stage[slot, pl.ds(pl.multiple_of(r * 32, 32), 32), :] = count.astype(jnp.int16)
            return inner

        lax.fori_loop(0, rows // 32, some_rows, 0)
        noise_copy(u).start()
        return carry

    take_resid.wait()

    def widen(r, carry):
        sl = pl.ds(pl.multiple_of(r * 32, 32), 32)
        total[sl, :] = back[sl, :].astype(jnp.float32) * (1.0 / scaling)
        return carry

    lax.fori_loop(0, tokens // 32, widen, 0)
    take_cot = pltpu.make_async_copy(cotangent, back, local_sem.at[0])
    take_cot.start()

    def multiply(slot, h):
        lhs = attn[:, pl.ds(pl.multiple_of(slot * rows, rows), rows)]

        def columns(j, carry):
            sl = pl.ds(pl.multiple_of(h * piece_width + j * 512, 512), 512)
            total[:, sl] += jnp.dot(lhs, weights[slot, :, sl], preferred_element_type=jnp.float32)
            return carry

        lax.fori_loop(0, piece_width // 512, columns, 0)

    def multiply_all(slots, h):
        def one(i, carry):
            slot = slots[-1][0]
            for k in range(len(slots) - 1):
                slot = jnp.where(i == k, slots[k][0], slot)
            wanted = slots[-1][1]
            for k in range(len(slots) - 1):
                wanted = jnp.where(i == k, slots[k][1], wanted)
            from_twin = lax.rem(slot, 2) != core

            @pl.when(wanted)
            def _():
                @pl.when(from_twin)
                def _():
                    wait_weight(slot, h)
                multiply(slot, h)
            return carry

        lax.fori_loop(0, len(slots), one, 0)

    always = place >= 0

    def multiply_own(h, carry):
        multiply_all([(shard, always), (twin, always)], h)
        return carry

    def gather_step(i, carry):
        t = lax.div(i, SLICES)
        h = lax.rem(i, SLICES)
        low = place - 1 - t
        high = place + 1 + t
        low_slot = jnp.maximum(low, 0) * 2 + core
        high_slot = jnp.minimum(high, last) * 2 + core

        @pl.when(low >= 0)
        def _():
            wait_weight(low_slot, h)
            pass_on(low_slot, h, t + 1, None)

        @pl.when(high <= last)
        def _():
            wait_weight(high_slot, h)
            pass_on(high_slot, h, None, t + 1)

        @pl.when(i == 0)
        def _():
            lax.fori_loop(0, SLICES, multiply_own, 0)

        steps = last * SLICES - 1
        lax.fori_loop(
            lax.div(units * jnp.minimum(i, steps), steps),
            lax.div(units * jnp.minimum(i + 1, steps), steps),
            noise_unit,
            0,
        )
        multiply_all([
            (low_slot, low >= 0),
            (high_slot, high <= last),
            (low_slot + 1 - 2 * core, low >= 0),
            (high_slot + 1 - 2 * core, high <= last),
        ], h)
        return carry

    lax.fori_loop(0, last * SLICES, gather_step, 0)
    noise_copy(units - 2).wait()
    noise_copy(units - 1).wait()

    def drain_weights(i, carry):
        t = lax.div(i, SLICES)
        h = lax.rem(i, SLICES)

        @pl.when((place < last) & (place - t >= 0))
        def _():
            weight_copy(shard, h, up_send.at[t, h], above).wait_send()

        @pl.when((place > 0) & (place + t <= last))
        def _():
            weight_copy(shard, h, down_send.at[t, h], below).wait_send()

        weight_copy(shard, h, core_send.at[t, h], twin).wait_send()
        return carry

    lax.fori_loop(0, line * SLICES, drain_weights, 0)

    take_cot.wait()
    span = 512

    def normalise(r, carry):
        sl = pl.ds(pl.multiple_of(r * 16, 16), 16)
        square = jnp.zeros((16, span), jnp.float32)
        cross = jnp.zeros((16, span), jnp.float32)
        for c in range(width // span):
            cs = pl.ds(c * span, span)
            value = total[sl, cs] * scaling
            upstream = gain[:, cs] * back[sl, cs].astype(jnp.float32)
            square = square + value * value
            cross = cross + value * upstream
        inverse = lax.rsqrt(jnp.sum(square, axis=-1, keepdims=True) * (1.0 / width) + norm_eps)
        slope = inverse * inverse * inverse * (
            jnp.sum(cross, axis=-1, keepdims=True) * (1.0 / width)
        )
        for c in range(width // span):
            cs = pl.ds(c * span, span)
            value = total[sl, cs] * scaling
            upstream = gain[:, cs] * back[sl, cs].astype(jnp.float32)
            back[sl, cs] = (inverse * upstream - value * slope).astype(jnp.bfloat16)
        return carry

    lax.fori_loop(0, tokens // 16, normalise, 0)

    def partial(block, piece):
        lhs = attn[:, pl.ds(pl.multiple_of(block * rows, rows), rows)]
        rhs = back[:, pl.ds(pl.multiple_of(piece * part, part), part)]
        return (
            lax.dot_general(lhs, rhs, (((0,), (0,)), ((), ())), preferred_element_type=jnp.float32)
            * scaling
        )

    def pair_copy(goal, piece):
        return pltpu.make_async_remote_copy(
            src_ref=weights.at[goal, :, pl.ds(pl.multiple_of(piece * part, part), part)],
            dst_ref=paired.at[goal, piece],
            send_sem=pair_send.at[goal, piece],
            recv_sem=pair_recv.at[goal, piece],
            device_id={"fsdp": twin},
            device_id_type=MESH,
        )

    def give_twin(i, piece):
        goal = i
        weights[goal, :, pl.ds(pl.multiple_of(piece * part, part), part)] = partial(
            goal * 2 + 1 - core, piece
        ).astype(jnp.bfloat16)
        pair_copy(goal, piece).start()
        return piece

    def chain_copy(goal, slot, piece, other):
        return pltpu.make_async_remote_copy(
            src_ref=chained.at[goal, piece],
            dst_ref=chained.at[slot, piece],
            send_sem=chain_send.at[goal, piece],
            recv_sem=chain_recv.at[slot, piece],
            device_id={"fsdp": other},
            device_id_type=MESH,
        )

    def own_term(goal, piece):
        pair_copy(goal, piece).wait_recv()
        return partial(goal * 2 + core, piece) + paired[goal, piece].astype(jnp.float32)

    def forward(goal, piece, first, slot, other):
        @pl.when(first)
        def _():
            chained[goal, piece] = own_term(goal, piece).astype(jnp.bfloat16)

        @pl.when(jnp.logical_not(first))
        def _():
            term = own_term(goal, piece)
            chain_copy(goal, goal, piece, other).wait_recv()
            chained[goal, piece] = (term + chained[goal, piece].astype(jnp.float32)).astype(
                jnp.bfloat16
            )

        chain_copy(goal, slot, piece, other).start()

    def group_copy(piece, step):
        cs = pl.ds(pl.multiple_of(piece * part, part), part)
        return pltpu.make_async_remote_copy(
            src_ref=ready.at[piece],
            dst_ref=out.at[group, :, cs],
            send_sem=group_send.at[step, piece],
            recv_sem=group_recv.at[group, piece],
            device_id={"sample": lax.rem(group + step, groups)},
            device_id_type=MESH,
        )

    def keep_copy(piece):
        cs = pl.ds(pl.multiple_of(piece * part, part), part)
        return pltpu.make_async_copy(
            ready.at[piece], out.at[group, :, cs], group_send.at[0, piece]
        )

    @pl.when(place == 0)
    def _():
        chained[0] = jnp.zeros(chained.shape[1:], chained.dtype)

    @pl.when(place == last)
    def _():
        chained[line] = jnp.zeros(chained.shape[1:], chained.dtype)

    lax.fori_loop(0, line, give_twin, 0)

    def reduce_step(step, carry):
        up_at = step - place
        up_piece = lax.div(jnp.maximum(up_at, 0), last)
        up_goal = last - lax.rem(jnp.maximum(up_at, 0), last)

        @pl.when((up_at >= 0) & (up_piece < PIECES) & (up_goal > place))
        def _():
            forward(up_goal, up_piece, place == 0, up_goal, above)

        down_at = step - (last - place)
        down_piece = lax.div(jnp.maximum(down_at, 0), last)
        down_goal = lax.rem(jnp.maximum(down_at, 0), last)

        @pl.when((down_at >= 0) & (down_piece < PIECES) & (down_goal < place))
        def _():
            slot = jnp.where(down_goal == place - 1, line, down_goal)
            forward(down_goal, down_piece, place == last, slot, below)

        turn = lax.div(step, last)

        @pl.when((lax.rem(step, last) == 0) & (turn < PIECES - 1))
        def _():
            lax.fori_loop(0, line, give_twin, turn + 1)

        @pl.when((lax.rem(step, last) == 0) & (turn >= 1))
        def _():
            piece = turn - 1
            term = own_term(place, piece)

            @pl.when(place > 0)
            def _():
                chain_copy(place, place, piece, below).wait_recv()

            @pl.when(place < last)
            def _():
                chain_copy(place, line, piece, above).wait_recv()

            ready[piece] = (
                term
                + chained[place, piece].astype(jnp.float32)
                + chained[line, piece].astype(jnp.float32)
            ).astype(jnp.bfloat16)
            for k in range(1, groups):
                group_copy(piece, k).start()
            keep_copy(piece).start()
        return carry

    lax.fori_loop(0, PIECES * last + 1, reduce_step, 0)

    def finish(piece, carry):
        def goals(goal, inner):
            pair_copy(goal, piece).wait_send()

            @pl.when(goal != place)
            def _():
                chain_copy(goal, goal, piece, above).wait_send()
            return inner

        lax.fori_loop(0, line, goals, 0)
        keep_copy(piece).wait()
        for k in range(1, groups):
            group_copy(piece, k).wait_send()
            source = lax.rem(group + k, groups)
            cs = pl.ds(pl.multiple_of(piece * part, part), part)
            pltpu.make_async_remote_copy(
                src_ref=ready.at[piece],
                dst_ref=out.at[source, :, cs],
                send_sem=group_send.at[k, piece],
                recv_sem=group_recv.at[source, piece],
                device_id={"sample": source},
                device_id_type=MESH,
            ).wait_recv()
        return carry

    lax.fori_loop(0, PIECES, finish, 0)


def exchange(seed_step, attn, resid, cotangent, gain, sampled, scaling):
    line = lax.axis_size("fsdp") // 2
    groups = lax.axis_size("sample")
    tokens, width = resid.shape
    rows = sampled.shape[0]
    part = width // PIECES
    vmem = pl.BlockSpec(memory_space=pltpu.VMEM)
    hbm = pl.BlockSpec(memory_space=pl.ANY)
    dma = pltpu.SemaphoreType.DMA
    return pl.pallas_call(
        functools.partial(exchange_kernel, line, groups, scaling),
        out_shape=(
            jax.ShapeDtypeStruct((groups, rows, width), jnp.bfloat16),
            jax.ShapeDtypeStruct((groups, rows, width), jnp.int16),
        ),
        in_specs=[pl.BlockSpec(memory_space=pltpu.SMEM), vmem, vmem, hbm, hbm, hbm],
        out_specs=(hbm, hbm),
        scratch_shapes=[
            pltpu.VMEM((2 * line, rows, width), jnp.bfloat16),
            pltpu.VMEM((tokens, width), jnp.bfloat16),
            pltpu.VMEM((tokens, width), jnp.float32),
            pltpu.VMEM((line, PIECES, rows, part), jnp.bfloat16),
            pltpu.VMEM((line + 1, PIECES, rows, part), jnp.bfloat16),
            pltpu.VMEM((PIECES, rows, part), jnp.bfloat16),
            pltpu.VMEM((2, rows, SPAN), jnp.int16),
            dma((2,)),
            dma((2,)),
            dma((2 * line, SLICES)),
            dma((line, SLICES)),
            dma((line, SLICES)),
            dma((line, SLICES)),
            dma((line, PIECES)),
            dma((line, PIECES)),
            dma((line, PIECES)),
            dma((line + 1, PIECES)),
            dma((groups, PIECES)),
            dma((groups, PIECES)),
        ],
        compiler_params=pltpu.CompilerParams(
            collective_id=0, has_side_effects=True, vmem_limit_bytes=60 * 2**20
        ),
    )(seed_step, attn, gain.astype(jnp.float32)[None, :], sampled, resid, cotangent)


def per_device(seed_step, attn, resid, cotangent, gain, mean, hess, momentum):
    own_rows = mean.shape[0]
    width = mean.shape[1]
    in_width = attn.shape[1]
    scaling = in_width ** (-0.5)
    groups = lax.axis_size("sample")
    group_id = lax.axis_index("sample")
    row_start = lax.axis_index("fsdp") * own_rows
    sigma = 1.0 / jnp.sqrt(ess_value * (hess + damping))
    epsilon = noise_table(seed_step, group_id, row_start, own_rows, in_width, width)
    sampled = (
        mean.astype(jnp.bfloat16).astype(jnp.float32)
        + sigma.astype(jnp.bfloat16).astype(jnp.float32) * epsilon
    ).astype(jnp.bfloat16)
    grads, counts = exchange(seed_step, attn, resid, cotangent, gain, sampled, scaling)
    grad_sum = jnp.zeros((own_rows, width), jnp.float32)
    curv_sum = jnp.zeros((own_rows, width), jnp.float32)
    for g in range(groups):
        grad = grads[g].astype(jnp.float32)
        noise = noise_scale * ((counts[g].astype(jnp.float32) + 1.0) / 4096.0 - 1.0)
        grad_sum = grad_sum + grad
        curv_sum = curv_sum + grad * noise
    return ivon_update(mean, hess, momentum, grad_sum, curv_sum / sigma, groups)


def solution(mesh):
    placed = (
        P(),
        P(("sample", "fsdp"), None),
        P(("sample", "fsdp"), None),
        P(("sample", "fsdp"), None),
        P(),
        P("fsdp", None),
        P("fsdp", None),
        P("fsdp", None),
    )
    return jax.shard_map(
        per_device,
        mesh=mesh,
        in_specs=placed,
        out_specs=(P("fsdp", None), P("fsdp", None), P("fsdp", None)),
        check_vma=False,
    )
```
